32 devices in a mesh: dom: 16 (over z, x, core), head: 2 (over y).
Axes of the slice: x: 2, y: 2, z: 4, core: 2. Of those that a mesh axis runs over, the one named last changes fastest.
Arguments:
- node_feats: bfloat16 [32768, 512], P(('dom', 'head')), may hold values from -16 to 16
- w_qkv: bfloat16 [512, 1536], replicated, may hold values from -1 to 1
- w_out: bfloat16 [512, 512], replicated, may hold values from -2 to 2
- neighbours: int32 [256, 4], P('dom'), may hold values from 0 to 15
- tiles: int32 [256, 4, 128, 128], P('dom'), may hold values 0 or 1
- partner: int32 [256], P('dom'), may hold values from 0 to 255, as said below
- layer_cot: bfloat16 [32768, 512], P(('dom', 'head')), may hold values from -6 to 6
Outputs:
- layer_out: bfloat16 [32768, 512], P(('dom', 'head'))
- feat_grad: bfloat16 [32768, 512], P(('dom', 'head'))
- dw_qkv: float32 [512, 1536], P('dom', 'head')
- dw_out: float32 [512, 512], P('head', 'dom')
The draws below stay inside these ranges and needn't reach their ends.
Inputs may be any that keep to these rules, and one draw needn't show every extreme that they name: partner is a perfect matching of the 256 node blocks: partner[partner[b]] = b, and the partner of a block lies in another part (part = block // 16). For every two parts, at most 2 blocks of one are matched to blocks of the other, and some two parts have exactly 2 such pairs.
All inputs are finite; a program needn't handle non-finite values. No bound on the sum of `tiles` on one device may be relied on, other than what follows from the above.
Results may differ from the reference program's by a relative error of at most 0.019.
The reference program's roundings to bfloat16 on the way count: a program that leaves them out, or rounds other values in their place, can miss the bound.
Values may be sent and summed in bfloat16 or wider, within the bound.
A program may use at most 192 MiB of HBM per device.

```python
import jax
import jax.numpy as jnp
from jax import lax

D = 512
H = 8
BS = 128
NBR = 4
GB = 4
BLK = 16
HG = 4
NB = 256
NODES = 32768
N_DOM = 16
N_HEAD = 2


def draw_partner(key, part):
    count = N_DOM
    key_labels, key_rounds, key_slots = jax.random.split(jax.random.fold_in(key, 7), 3)
    labels = jax.random.permutation(key_labels, count).astype(jnp.int32)
    inverse = jnp.zeros((count,), jnp.int32).at[labels].set(jnp.arange(count, dtype=jnp.int32))
    rounds = jax.random.permutation(key_rounds, count - 1).astype(jnp.int32)
    chosen = rounds[jnp.arange(BLK, dtype=jnp.int32) % (count - 1)]
    label_col = labels[:, None]
    round_row = chosen[None, :]
    other = jnp.where(label_col == count - 1, round_row, jnp.where(label_col == round_row, count - 1, (2 * round_row - label_col) % (count - 1)))
    partner_part = inverse[other]
    slot_keys = jax.random.split(key_slots, count)
    slot_table = jax.vmap(lambda single: jax.random.permutation(single, BLK))(slot_keys).astype(jnp.int32)
    columns = jnp.broadcast_to(jnp.arange(BLK, dtype=jnp.int32)[None, :], (count, BLK))
    partner_slot = slot_table[partner_part, columns]
    matched = partner_part * BLK + partner_slot
    row_ids = jnp.broadcast_to(jnp.arange(count, dtype=jnp.int32)[:, None], (count, BLK))
    result = jnp.zeros((count, BLK), jnp.int32).at[row_ids, slot_table].set(matched)
    return result.reshape(count * BLK)


def draw_node_feats(key, part):
    base = jax.random.fold_in(key, 11)
    key_noise = jax.random.fold_in(base, 0)
    result = jnp.clip(jax.random.normal(key_noise, (NODES, D), jnp.float32), -6.0, 6.0)
    return result.astype(jnp.bfloat16)


def draw_w_qkv(key, part):
    base = jax.random.fold_in(key, 13)
    raw = jnp.clip(jax.random.normal(base, (D, N_HEAD, 3, D // N_HEAD), jnp.float32), -4.0, 4.0) * D ** (-0.5)
    return raw.reshape(D, 3 * D).astype(jnp.bfloat16)


def set_ends(drawn, rng, smallest, high):
    place = [jax.random.randint(jax.random.fold_in(rng, axis), (), 0, length) for axis, length in enumerate(drawn.shape)]
    widest = drawn.shape.index(max(drawn.shape))
    neighbour = place[:widest] + [(place[widest] + 1) % drawn.shape[widest]] + place[widest + 1:]
    return drawn.at[tuple(place)].set(smallest).at[tuple(neighbour)].set(high)


def block_levels(stream_key, extent, pieces, low, high):
    factor_of, own = 1.0, jax.random.fold_in(stream_key, 6)
    for dim, shards_of in pieces:
        heights = jnp.exp(jax.random.uniform(jax.random.fold_in(own, dim), (shards_of,), jnp.float32, low / len(pieces), high / len(pieces)))
        factor_of = factor_of * jnp.repeat(heights, extent[dim] // shards_of).reshape([-1 if axis == dim else 1 for axis in range(len(extent))])
    return factor_of


def normal_values(rng, shape, spread, most, cuts=(), held_as=jnp.bfloat16):
    drawn = jax.random.normal(rng, shape, jnp.float32) * spread
    if len(cuts) > 0:
        drawn = block_levels(rng, shape, cuts, -0.22, 0.18) * drawn
    return jnp.clip(drawn, min=-most, max=most).astype(held_as)


def setup_inputs(seed: int = 0) -> dict:
    arg_keys = jax.random.split(jax.random.key(seed), 8)
    return {
        "node_feats": draw_node_feats(jax.random.fold_in(arg_keys[7], 71), 0),
        "w_qkv": draw_w_qkv(jax.random.fold_in(arg_keys[7], 71), 0),
        "w_out": normal_values(arg_keys[2], (D, D), (max(D // 64, 1)) ** -0.5, 2.0),
        "neighbours": set_ends(jax.random.randint(arg_keys[3], (NB, NBR), 0, BLK), jax.random.fold_in(arg_keys[3], 1), 0, BLK - 1).astype(jnp.int32),
        "tiles": set_ends((jax.random.randint(arg_keys[4], (NB, NBR, BS, BS), 0, 2) < 1).astype(jnp.int32), jax.random.fold_in(arg_keys[4], 1), 0, 1),
        "partner": draw_partner(jax.random.fold_in(arg_keys[7], 71), 0),
        "layer_cot": normal_values(arg_keys[6], (NODES, D), 1.0, 6.0, ((0, 32),)),
    }


def reference(node_feats, w_qkv, w_out, neighbours, tiles, partner, layer_cot):
    head_dim = D // H
    scale = head_dim ** -0.5
    qkv = jnp.dot(node_feats, w_qkv, preferred_element_type=jnp.float32).astype(jnp.bfloat16)
    split = qkv.reshape(NB, BS, N_HEAD, 3, HG * head_dim)
    queries = split[:, :, :, 0].reshape(NB, BS, H, head_dim)
    keys = split[:, :, :, 1].reshape(NB, BS, H, head_dim)
    values = split[:, :, :, 2].reshape(NB, BS, H, head_dim)
    cot_attn = jnp.dot(layer_cot, w_out.T, preferred_element_type=jnp.float32).astype(jnp.bfloat16)
    cot_attn = cot_attn.reshape(NB, BS, H, head_dim)
    block_base = (jnp.arange(NB, dtype=jnp.int32) // BLK) * BLK
    key_ids = jnp.concatenate([block_base[:, None] + neighbours, partner[:, None]], axis=1).astype(jnp.int32)

    def attend(carry, start):
        key_grads, value_grads = carry
        ids = lax.dynamic_slice_in_dim(key_ids, start, GB, 0)
        query_block = lax.dynamic_slice_in_dim(queries, start, GB, 0).astype(jnp.float32)
        key_block = keys[ids].reshape(GB, (NBR + 1) * BS, H, head_dim).astype(jnp.float32)
        value_block = values[ids].reshape(GB, (NBR + 1) * BS, H, head_dim).astype(jnp.float32)
        tile_block = lax.dynamic_slice_in_dim(tiles, start, GB, 0)
        visible = jnp.concatenate([tile_block.transpose(0, 2, 1, 3).reshape(GB, BS, NBR * BS) != 0,
                                   jnp.ones((GB, BS, BS), dtype=jnp.bool_)], axis=2)
        scores = jnp.einsum('bqhd,bkhd->bhqk', query_block, key_block) * scale
        scores = jnp.where(visible[:, None], scores, -1e30)
        peak = jnp.max(scores, axis=-1, keepdims=True)
        total = jnp.sum(jnp.exp(scores - peak), axis=-1, keepdims=True)
        probs = jnp.exp(scores - peak) / total
        probs_low = probs.astype(jnp.bfloat16).astype(jnp.float32)
        attended = jnp.einsum('bhqk,bkhd->bqhd', probs_low, value_block).astype(jnp.bfloat16)
        grad_block = lax.dynamic_slice_in_dim(cot_attn, start, GB, 0).astype(jnp.float32)
        delta = jnp.sum(grad_block * attended.astype(jnp.float32), axis=-1).transpose(0, 2, 1)
        grad_values = jnp.einsum('bhqk,bqhd->bkhd', probs_low, grad_block)
        grad_probs = jnp.einsum('bqhd,bkhd->bhqk', grad_block, value_block)
        grad_scores = (probs * (grad_probs - delta[..., None]) * scale).astype(jnp.bfloat16).astype(jnp.float32)
        grad_query = jnp.einsum('bhqk,bkhd->bqhd', grad_scores, key_block)
        grad_keys = jnp.einsum('bhqk,bqhd->bkhd', grad_scores, query_block)
        near_ids = ids[:, :NBR].reshape(-1)
        near_keys = grad_keys[:, :NBR * BS].reshape(GB * NBR, BS, D)
        near_values = grad_values[:, :NBR * BS].reshape(GB * NBR, BS, D)
        key_grads = key_grads.at[near_ids].add(near_keys)
        value_grads = value_grads.at[near_ids].add(near_values)
        far_term = jnp.concatenate([grad_keys[:, NBR * BS:].reshape(GB, BS, D),
                                    grad_values[:, NBR * BS:].reshape(GB, BS, D)], axis=-1).astype(jnp.bfloat16)
        return (key_grads, value_grads), (attended.reshape(GB, BS, D), grad_query.reshape(GB, BS, D), far_term)

    starts = jnp.arange(0, NB, GB, dtype=jnp.int32)
    zero_grads = jnp.zeros((NB, BS, D), jnp.float32)
    (key_grads, value_grads), (attended, grad_query, far_term) = lax.scan(attend, (zero_grads, zero_grads), starts)
    far_term = lax.optimization_barrier(far_term.reshape(NB, BS, 2 * D))
    partner_term = far_term[partner].astype(jnp.float32)
    key_grads = key_grads + partner_term[..., :D]
    value_grads = value_grads + partner_term[..., D:]
    attended = attended.reshape(NODES, D)
    layer_out = jnp.dot(attended, w_out, preferred_element_type=jnp.float32).astype(jnp.bfloat16)
    stacked = jnp.stack([grad_query.reshape(NB, BS, N_HEAD, HG * head_dim),
                         key_grads.reshape(NB, BS, N_HEAD, HG * head_dim),
                         value_grads.reshape(NB, BS, N_HEAD, HG * head_dim)], axis=3)
    dqkv = stacked.reshape(NODES, 3 * D).astype(jnp.bfloat16)
    feat_grad = jnp.dot(dqkv, w_qkv.T, preferred_element_type=jnp.float32).astype(jnp.bfloat16)
    dw_qkv = jnp.dot(node_feats.T, dqkv, preferred_element_type=jnp.float32)
    dw_out = jnp.dot(attended.T, layer_cot, preferred_element_type=jnp.float32)
    return (layer_out, feat_grad, dw_qkv, dw_out)
```

```python
import jax
import jax.numpy as jnp
from jax import lax
from jax.experimental import pallas as pl
from jax.experimental.pallas import tpu as pltpu
from jax.sharding import PartitionSpec as P

H = 8
NBR = 4
F32 = jnp.float32
BF16 = jnp.bfloat16


def attention_kernel(near_ref, q_ref, c_ref, kv_ref, far_ref, tile_ref,
                     att_ref, dq_ref, dnear_ref, dfar_ref, acc_ref, bias_ref):
    step = pl.program_id(0)
    block_size, width = q_ref.shape[1], q_ref.shape[2]
    head_dim = width // H
    pair = 2 * head_dim
    reach = (NBR + 1) * block_size
    scale = head_dim ** (-0.5)

    @pl.when(step == 0)
    def _():
        acc_ref[...] = jnp.zeros_like(acc_ref)

    for j in range(NBR):
        bias_ref[:, j * block_size:(j + 1) * block_size] = jnp.where(tile_ref[0, j] != 0, 0.0, -1e30).astype(F32)
    bias_ref[:, NBR * block_size:] = jnp.zeros((block_size, block_size), F32)
    ids = [near_ref[step * NBR + j] for j in range(NBR)]
    first = lax.broadcasted_iota(jnp.int32, (block_size, pair), 1) < head_dim

    def stacked(x):
        zero = jnp.zeros_like(x)
        return jnp.concatenate([jnp.where(first, x, zero), jnp.where(first, zero, x)], axis=0)

    def joined(column):
        cols = pl.ds(column, pair)
        return jnp.concatenate([kv_ref[i, :, cols] for i in ids] + [far_ref[0, :, cols]], axis=0)

    last = (((1,), (1,)), ((), ()))
    lead = (((0,), (0,)), ((), ()))
    for p in range(H // 2):
        low = p * pair
        cols = slice(low, low + pair)
        query = stacked(q_ref[0, :, cols].astype(F32) * scale).astype(BF16)
        cot_pair = c_ref[0, :, cols].astype(F32)
        cot32 = stacked(cot_pair)
        cot = cot32.astype(BF16)
        keys = joined(low)
        values = joined(width + low)
        scores = lax.dot_general(query, keys, last, preferred_element_type=F32)
        bias = bias_ref[...]
        scores = scores + jnp.concatenate([bias, bias], axis=0)
        peak = jnp.max(scores, axis=-1, keepdims=True)
        weight = jnp.exp(scores - peak)
        total = jnp.sum(weight, axis=-1, keepdims=True)
        probs = weight * (1.0 / total)
        low_probs = probs.astype(BF16)
        att2 = jnp.dot(low_probs, values, preferred_element_type=F32).astype(BF16).astype(F32)
        att_ref[0, :, cols] = jnp.where(first, att2[:block_size], att2[block_size:]).astype(BF16)
        delta = jnp.sum(cot32 * att2, axis=-1, keepdims=True)
        grad_probs = lax.dot_general(cot, values, last, preferred_element_type=F32)
        dscores = (probs * (grad_probs - delta)).astype(BF16)
        dq2 = jnp.dot(dscores, keys, preferred_element_type=F32) * scale
        dq_ref[0, :, cols] = jnp.where(first, dq2[:block_size], dq2[block_size:]).astype(BF16)
        dk = lax.dot_general(query, dscores, lead, preferred_element_type=F32)
        dv = lax.dot_general(cot, low_probs, lead, preferred_element_type=F32)
        for base, grad in ((low, dk), (width + low, dv)):
            rows = pl.ds(base, pair)
            for j in range(NBR):
                acc_ref[ids[j], rows, :] += grad[:, j * block_size:(j + 1) * block_size]
            dfar_ref[0, rows, :] = grad[:, NBR * block_size:].astype(BF16)

    @pl.when(step == pl.num_programs(0) - 1)
    def _():
        dnear_ref[...] = acc_ref[...].astype(BF16)


def attention(near_ids, offset, query, cot, kv, kv_far, tiles):
    own, block_size, width = query.shape
    blocks = kv.shape[0]
    scalars = jnp.concatenate([near_ids.reshape(-1), offset.reshape(1)])
    count = own * NBR
    row = lambda b, s: (b, 0, 0)
    whole = lambda b, s: (0, 0, 0)
    grid_spec = pltpu.PrefetchScalarGridSpec(
        num_scalar_prefetch=1,
        grid=(own,),
        in_specs=[
            pl.BlockSpec((1, block_size, width), row),
            pl.BlockSpec((1, block_size, width), row),
            pl.BlockSpec((blocks, block_size, 2 * width), whole),
            pl.BlockSpec((1, block_size, 2 * width), row),
            pl.BlockSpec((1, NBR, block_size, block_size), lambda b, s: (s[count] + b, 0, 0, 0)),
        ],
        out_specs=[
            pl.BlockSpec((1, block_size, width), row),
            pl.BlockSpec((1, block_size, width), row),
            pl.BlockSpec((blocks, 2 * width, block_size), whole),
            pl.BlockSpec((1, 2 * width, block_size), row),
        ],
        scratch_shapes=[
            pltpu.VMEM((blocks, 2 * width, block_size), F32),
            pltpu.VMEM((block_size, (NBR + 1) * block_size), F32),
        ],
    )
    flops = 12 * own * H * block_size * (NBR + 1) * block_size * (width // H)
    return pl.pallas_call(
        attention_kernel,
        grid_spec=grid_spec,
        out_shape=[
            jax.ShapeDtypeStruct((own, block_size, width), BF16),
            jax.ShapeDtypeStruct((own, block_size, width), BF16),
            jax.ShapeDtypeStruct((blocks, 2 * width, block_size), BF16),
            jax.ShapeDtypeStruct((own, 2 * width, block_size), BF16),
        ],
        compiler_params=pltpu.CompilerParams(vmem_limit_bytes=56 * 1024 * 1024),
        cost_estimate=pl.CostEstimate(
            flops=8 * flops,
            bytes_accessed=20 * own * block_size * width,
            transcendentals=own * H * block_size * (NBR + 1) * block_size,
        ),
        name="attention",
    )(scalars, query, cot, kv, kv_far, tiles)


def body(node_feats, w_qkv, w_out, neighbours, tiles, partner, layer_cot):
    rows, width = node_feats.shape
    parts = lax.axis_size("dom")
    groups = lax.axis_size("head")
    me = lax.axis_index("head")
    blocks = partner.shape[0]
    block_size = tiles.shape[2]
    own = blocks // groups
    half = block_size // 2
    span = width // groups
    slots = (blocks + parts - 2) // (parts - 1)
    swap = [(0, 1), (1, 0)]

    def pick(x, i):
        return lax.dynamic_index_in_dim(x, i, 1, keepdims=False)

    def halves(mine, other):
        both = jnp.stack([mine, other], axis=1)
        flip = jnp.stack([other, mine], axis=1)
        return jnp.where(me == 0, both, flip).reshape(mine.shape[0], block_size, -1)

    target = partner // blocks
    iota = jnp.arange(blocks, dtype=jnp.int32)
    same = target[:, None] == target[None, :]
    earlier = iota[None, :] < iota[:, None]
    lower = partner[None, :] < partner[:, None]
    order = (iota + own * me) % blocks
    send_slot = (target * slots + jnp.sum((same & earlier).astype(jnp.int32), axis=1))[order]
    recv_slot = (target * slots + jnp.sum((same & lower).astype(jnp.int32), axis=1))[order]
    all_slots = jnp.arange(parts * slots, dtype=jnp.int32)
    send_from = jnp.sum(jnp.where(send_slot[None, :] == all_slots[:, None], iota[None, :], 0), axis=1)
    recv_from = jnp.sum(jnp.where(recv_slot[None, :] == all_slots[:, None], iota[None, :], 0), axis=1)

    feats = node_feats.reshape(own, 2, half, width)
    peer_a = lax.ppermute(pick(feats, 1 - me), "head", swap)
    peer_b = lax.ppermute(pick(feats, me), "head", swap)
    half_feats = jnp.concatenate([pick(feats, me), peer_a], axis=0)
    incoming = lax.all_to_all(half_feats[send_from], "dom", split_axis=0, concat_axis=0, tiled=True)
    half_far = incoming[recv_slot]
    other_far = lax.ppermute(half_far[own:], "head", swap)
    feats_far = halves(half_far[:own], other_far)
    feats_peer = halves(peer_a, peer_b)

    w_split = w_qkv.reshape(width, groups, 3, span).transpose(0, 2, 1, 3).reshape(width, 3 * width)
    w_query, w_kv = w_split[:, :width], w_split[:, width:]

    def project(x, w):
        return jnp.dot(x, w, preferred_element_type=F32).astype(BF16)

    query = project(node_feats, w_query).reshape(own, block_size, width)
    cot = project(layer_cot, w_out.T).reshape(own, block_size, width)
    feats_near = jnp.concatenate([node_feats, feats_peer.reshape(rows, width)], axis=0)
    feats_far = feats_far.reshape(rows, width)
    kv = project(feats_near, w_kv).reshape(blocks, block_size, 2 * width)
    kv_far = project(feats_far, w_kv).reshape(own, block_size, 2 * width)
    near_ids = lax.dynamic_slice_in_dim(neighbours, me * own, own, 0)
    near_ids = (near_ids + own * me) % blocks
    attended, dq, dnear, dfar = attention(near_ids, me * own, query, cot, kv, kv_far, tiles)

    attended = attended.reshape(rows, width)
    dq = dq.reshape(rows, width)

    def back(x):
        return jnp.einsum("bcn,dc->bnd", x, w_kv, preferred_element_type=F32)

    far_grad = back(dfar).astype(BF16).reshape(own, 2, half, width)
    far_peer = lax.ppermute(pick(far_grad, 1 - me), "head", swap)
    half_grad = jnp.concatenate([pick(far_grad, me), far_peer], axis=0)
    returned = lax.all_to_all(half_grad[recv_from], "dom", split_axis=0, concat_axis=0, tiled=True)
    returned = returned[send_slot].astype(F32)

    peer_grad = back(dnear[own:]).reshape(own, 2, half, width)
    early = lax.ppermute(pick(peer_grad, 1 - me).astype(BF16), "head", swap)
    late = lax.ppermute((pick(peer_grad, me) + returned[own:]).astype(BF16), "head", swap)

    def rows_in(spec, a, b):
        return jnp.einsum(spec, a, b, preferred_element_type=F32)

    dw_q = rows_in("rd,rc->dc", node_feats, dq)
    dw_kv = rows_in("bnd,bcn->dc", feats_near.reshape(blocks, block_size, width), dnear)
    dw_kv = dw_kv + rows_in("bnd,bcn->dc", feats_far.reshape(own, block_size, width), dfar)
    dw_all = jnp.concatenate([dw_q, dw_kv], axis=1).reshape(width, 3, groups, span)
    dw_out = rows_in("rc,rd->cd", layer_cot, attended).reshape(width, groups, span)

    def group_of(i):
        qkv = lax.dynamic_index_in_dim(dw_all, i, 2, keepdims=False).reshape(width, 3 * span)
        return jnp.concatenate([qkv, lax.dynamic_index_in_dim(dw_out, i, 1, keepdims=False)], axis=1)

    dw_peer = lax.ppermute(group_of(1 - me).astype(BF16), "head", swap)
    dw_mine = (group_of(me) + dw_peer.astype(F32)).astype(BF16)
    dw_parts = lax.all_to_all(
        dw_mine.reshape(parts, width // parts, 4 * span), "dom", split_axis=0, concat_axis=0, tiled=True
    )
    dw_sum = jnp.sum(dw_parts.astype(F32), axis=0)

    layer_out = project(attended, w_out)
    own_grad = (
        jnp.einsum("rc,dc->rd", dq, w_query, preferred_element_type=F32).reshape(own, block_size, width)
        + back(dnear[:own])
    )
    feat_grad = own_grad + halves(returned[:own] + early.astype(F32), late.astype(F32))
    feat_grad = feat_grad.astype(BF16).reshape(rows, width)
    return (layer_out, feat_grad, dw_sum[:, : 3 * span], dw_sum[:, 3 * span:].T)


def solution(mesh):
    placed = (
        P(("dom", "head"), None),
        P(),
        P(),
        P("dom", None),
        P("dom", None, None, None),
        P("dom"),
        P(("dom", "head"), None),
    )
    return jax.shard_map(
        body,
        mesh=mesh,
        in_specs=placed,
        out_specs=(
            P(("dom", "head"), None),
            P(("dom", "head"), None),
            P("dom", "head"),
            P("head", "dom"),
        ),
        check_vma=False,
    )
```

```python
import jax
import jax.numpy as jnp
from jax import lax
from jax.experimental import pallas as pl
from jax.experimental.pallas import tpu as pltpu
from jax.sharding import PartitionSpec as P

H = 8
NBR = 4
F32 = jnp.float32
BF16 = jnp.bfloat16


def attention_kernel(near_ref, q_ref, c_ref, kv_ref, far_ref, tile_ref,
                     att_ref, dq_ref, dnear_ref, dfar_ref, acc_ref, bias_ref):
    step = pl.program_id(0)
    block_size, width = q_ref.shape[1], q_ref.shape[2]
    head_dim = width // H
    pair = 2 * head_dim
    reach = (NBR + 1) * block_size
    scale = head_dim ** (-0.5)

    @pl.when(step == 0)
    def _():
        acc_ref[...] = jnp.zeros_like(acc_ref)

    for j in range(NBR):
        bias_ref[:, j * block_size:(j + 1) * block_size] = jnp.where(tile_ref[0, j] != 0, 0.0, -1e30).astype(F32)
    bias_ref[:, NBR * block_size:] = jnp.zeros((block_size, block_size), F32)
    ids = [near_ref[step * NBR + j] for j in range(NBR)]
    first = lax.broadcasted_iota(jnp.int32, (block_size, pair), 1) < head_dim

    def stacked(x):
        zero = jnp.zeros_like(x)
        return jnp.concatenate([jnp.where(first, x, zero), jnp.where(first, zero, x)], axis=0)

    def joined(column):
        cols = pl.ds(column, pair)
        return jnp.concatenate([kv_ref[i, :, cols] for i in ids] + [far_ref[0, :, cols]], axis=0)

    last = (((1,), (1,)), ((), ()))
    lead = (((0,), (0,)), ((), ()))
    for p in range(H // 2):
        low = p * pair
        cols = slice(low, low + pair)
        query = stacked(q_ref[0, :, cols].astype(F32) * scale).astype(BF16)
        cot_pair = c_ref[0, :, cols].astype(F32)
        cot32 = stacked(cot_pair)
        cot = cot32.astype(BF16)
        keys = joined(low)
        values = joined(width + low)
        scores = lax.dot_general(query, keys, last, preferred_element_type=F32)
        bias = bias_ref[...]
        scores = scores + jnp.concatenate([bias, bias], axis=0)
        peak = jnp.max(scores, axis=-1, keepdims=True)
        weight = jnp.exp(scores - peak)
        total = jnp.sum(weight, axis=-1, keepdims=True)
        probs = weight * (1.0 / total)
        low_probs = probs.astype(BF16)
        att2 = jnp.dot(low_probs, values, preferred_element_type=F32).astype(BF16).astype(F32)
        att_ref[0, :, cols] = jnp.where(first, att2[:block_size], att2[block_size:]).astype(BF16)
        delta = jnp.sum(cot32 * att2, axis=-1, keepdims=True)
        grad_probs = lax.dot_general(cot, values, last, preferred_element_type=F32)
        dscores = (probs * (grad_probs - delta)).astype(BF16)
        dq2 = jnp.dot(dscores, keys, preferred_element_type=F32) * scale
        dq_ref[0, :, cols] = jnp.where(first, dq2[:block_size], dq2[block_size:]).astype(BF16)
        dk = lax.dot_general(query, dscores, lead, preferred_element_type=F32)
        dv = lax.dot_general(cot, low_probs, lead, preferred_element_type=F32)
        for base, grad in ((low, dk), (width + low, dv)):
            rows = pl.ds(base, pair)
            for j in range(NBR):
                acc_ref[ids[j], rows, :] += grad[:, j * block_size:(j + 1) * block_size]
            dfar_ref[0, rows, :] = grad[:, NBR * block_size:].astype(BF16)

    @pl.when(step == pl.num_programs(0) - 1)
    def _():
        dnear_ref[...] = acc_ref[...].astype(BF16)


def attention(near_ids, offset, query, cot, kv, kv_far, tiles):
    own, block_size, width = query.shape
    blocks = kv.shape[0]
    scalars = jnp.concatenate([near_ids.reshape(-1), offset.reshape(1)])
    count = own * NBR
    row = lambda b, s: (b, 0, 0)
    whole = lambda b, s: (0, 0, 0)
    grid_spec = pltpu.PrefetchScalarGridSpec(
        num_scalar_prefetch=1,
        grid=(own,),
        in_specs=[
            pl.BlockSpec((1, block_size, width), row),
            pl.BlockSpec((1, block_size, width), row),
            pl.BlockSpec((blocks, block_size, 2 * width), whole),
            pl.BlockSpec((1, block_size, 2 * width), row),
            pl.BlockSpec((1, NBR, block_size, block_size), lambda b, s: (s[count] + b, 0, 0, 0)),
        ],
        out_specs=[
            pl.BlockSpec((1, block_size, width), row),
            pl.BlockSpec((1, block_size, width), row),
            pl.BlockSpec((blocks, 2 * width, block_size), whole),
            pl.BlockSpec((1, 2 * width, block_size), row),
        ],
        scratch_shapes=[
            pltpu.VMEM((blocks, 2 * width, block_size), F32),
            pltpu.VMEM((block_size, (NBR + 1) * block_size), F32),
        ],
    )
    flops = 12 * own * H * block_size * (NBR + 1) * block_size * (width // H)
    return pl.pallas_call(
        attention_kernel,
        grid_spec=grid_spec,
        out_shape=[
            jax.ShapeDtypeStruct((own, block_size, width), BF16),
            jax.ShapeDtypeStruct((own, block_size, width), BF16),
            jax.ShapeDtypeStruct((blocks, 2 * width, block_size), BF16),
            jax.ShapeDtypeStruct((own, 2 * width, block_size), BF16),
        ],
        compiler_params=pltpu.CompilerParams(vmem_limit_bytes=56 * 1024 * 1024),
        cost_estimate=pl.CostEstimate(
            flops=8 * flops,
            bytes_accessed=20 * own * block_size * width,
            transcendentals=own * H * block_size * (NBR + 1) * block_size,
        ),
        name="attention",
    )(scalars, query, cot, kv, kv_far, tiles)


def body(node_feats, w_qkv, w_out, neighbours, tiles, partner, layer_cot):
    rows, width = node_feats.shape
    parts = lax.axis_size("dom")
    groups = lax.axis_size("head")
    me = lax.axis_index("head")
    blocks = partner.shape[0]
    block_size = tiles.shape[2]
    own = blocks // groups
    half = block_size // 2
    span = width // groups
    slots = (blocks + parts - 2) // (parts - 1)
    swap = [(0, 1), (1, 0)]

    def pick(x, i):
        return lax.dynamic_index_in_dim(x, i, 1, keepdims=False)

    def halves(mine, other):
        both = jnp.stack([mine, other], axis=1)
        flip = jnp.stack([other, mine], axis=1)
        return jnp.where(me == 0, both, flip).reshape(mine.shape[0], block_size, -1)

    target = partner // blocks
    iota = jnp.arange(blocks, dtype=jnp.int32)
    same = target[:, None] == target[None, :]
    earlier = iota[None, :] < iota[:, None]
    lower = partner[None, :] < partner[:, None]
    order = (iota + own * me) % blocks
    send_slot = (target * slots + jnp.sum((same & earlier).astype(jnp.int32), axis=1))[order]
    recv_slot = (target * slots + jnp.sum((same & lower).astype(jnp.int32), axis=1))[order]
    all_slots = jnp.arange(parts * slots, dtype=jnp.int32)
    send_from = jnp.sum(jnp.where(send_slot[None, :] == all_slots[:, None], iota[None, :], 0), axis=1)
    recv_from = jnp.sum(jnp.where(recv_slot[None, :] == all_slots[:, None], iota[None, :], 0), axis=1)

    feats = node_feats.reshape(own, 2, half, width)
    peer_a = lax.ppermute(pick(feats, 1 - me), "head", swap)
    peer_b = lax.ppermute(pick(feats, me), "head", swap)
    half_feats = jnp.concatenate([pick(feats, me), peer_a], axis=0)
    incoming = lax.all_to_all(half_feats[send_from], "dom", split_axis=0, concat_axis=0, tiled=True)
    half_far = incoming[recv_slot]
    other_far = lax.ppermute(half_far[own:], "head", swap)
    feats_far = halves(half_far[:own], other_far)
    feats_peer = halves(peer_a, peer_b)

    w_split = w_qkv.reshape(width, groups, 3, span).transpose(0, 2, 1, 3).reshape(width, 3 * width)
    w_query, w_kv = w_split[:, :width], w_split[:, width:]

    def project(x, w):
        return jnp.dot(x, w, preferred_element_type=F32).astype(BF16)

    query = project(node_feats, w_query).reshape(own, block_size, width)
    cot = project(layer_cot, w_out.T).reshape(own, block_size, width)
    feats_near = jnp.concatenate([node_feats, feats_peer.reshape(rows, width)], axis=0)
    feats_far = feats_far.reshape(rows, width)
    kv = project(feats_near, w_kv).reshape(blocks, block_size, 2 * width)
    kv_far = project(feats_far, w_kv).reshape(own, block_size, 2 * width)
    near_ids = lax.dynamic_slice_in_dim(neighbours, me * own, own, 0)
    near_ids = (near_ids + own * me) % blocks
    attended, dq, dnear, dfar = attention(near_ids, me * own, query, cot, kv, kv_far, tiles)

    attended = attended.reshape(rows, width)
    dq = dq.reshape(rows, width)

    def back(x):
        return jnp.einsum("bcn,dc->bnd", x, w_kv, preferred_element_type=F32)

    core = lax.axis_index("dom") % 2
    chip_swap = [(i, i ^ 1) for i in range(parts)]
    same_core = [[i for i in range(parts) if i % 2 == c] for c in range(2)]

    def rows_in(spec, a, b):
        return jnp.einsum(spec, a, b, preferred_element_type=F32)

    near_rows = feats_near.reshape(blocks, block_size, width)
    far_rows = feats_far.reshape(own, block_size, width)
    near_split = dnear.reshape(blocks, 2, groups, span, block_size)
    far_split = dfar.reshape(own, 2, groups, span, block_size)

    def group_of(i):
        cols = lambda x: lax.dynamic_slice_in_dim(x, i * span, span, 1)
        dw_q = rows_in("rd,rc->dc", node_feats, cols(dq))
        near = lax.dynamic_index_in_dim(near_split, i, 2, keepdims=False).reshape(blocks, 2 * span, block_size)
        far = lax.dynamic_index_in_dim(far_split, i, 2, keepdims=False).reshape(own, 2 * span, block_size)
        dw_kv = rows_in("bnd,bcn->dc", near_rows, near) + rows_in("bnd,bcn->dc", far_rows, far)
        dw_out = rows_in("rc,rd->cd", layer_cot, cols(attended))
        return dw_q, dw_kv, dw_out

    far_grad = back(dfar).astype(BF16).reshape(own, 2, half, width)
    far_peer = lax.ppermute(pick(far_grad, 1 - me), "head", swap)
    dw_send = jnp.concatenate([x.astype(BF16) for x in group_of(1 - me)], axis=1)
    peer_grad = back(dnear[own:]).reshape(own, 2, half, width)
    early_send = pick(peer_grad, 1 - me).astype(BF16)
    far_peer, dw_send, early_send = lax.optimization_barrier((far_peer, dw_send, early_send))
    half_grad = jnp.concatenate([pick(far_grad, me), far_peer], axis=0)
    returned = lax.all_to_all(half_grad[recv_from], "dom", split_axis=0, concat_axis=0, tiled=True)
    dw_peer = lax.ppermute(dw_send, "head", swap)
    early = lax.ppermute(early_send, "head", swap)

    dw_mine = jnp.concatenate(group_of(me), axis=1) + dw_peer.astype(F32)
    dw_mine = dw_mine.reshape(parts // 2, 2, width // parts, 4 * span)
    dw_core = lax.ppermute(pick(dw_mine, 1 - core).astype(BF16), "dom", chip_swap)
    dw_half = (pick(dw_mine, core) + dw_core.astype(F32)).astype(BF16)
    returned, dw_half = lax.optimization_barrier((returned, dw_half))

    returned = returned[send_slot].astype(F32)
    late = lax.ppermute((pick(peer_grad, me) + returned[own:]).astype(BF16), "head", swap)
    dw_parts = lax.all_to_all(
        dw_half, "dom", split_axis=0, concat_axis=0, tiled=True, axis_index_groups=same_core
    )
    dw_sum = jnp.sum(dw_parts.astype(F32), axis=0)

    layer_out = project(attended, w_out)
    own_grad = (
        jnp.einsum("rc,dc->rd", dq, w_query, preferred_element_type=F32).reshape(own, block_size, width)
        + back(dnear[:own])
    )
    feat_grad = own_grad + halves(returned[:own] + early.astype(F32), late.astype(F32))
    feat_grad = feat_grad.astype(BF16).reshape(rows, width)
    return (layer_out, feat_grad, dw_sum[:, : 3 * span], dw_sum[:, 3 * span:].T)


def solution(mesh):
    placed = (
        P(("dom", "head"), None),
        P(),
        P(),
        P("dom", None),
        P("dom", None, None, None),
        P("dom"),
        P(("dom", "head"), None),
    )
    return jax.shard_map(
        body,
        mesh=mesh,
        in_specs=placed,
        out_specs=(
            P(("dom", "head"), None),
            P(("dom", "head"), None),
            P("dom", "head"),
            P("head", "dom"),
        ),
        check_vma=False,
    )
```

```python
import jax
import jax.numpy as jnp
from jax import lax
from jax.experimental import pallas as pl
from jax.experimental.pallas import tpu as pltpu
from jax.sharding import PartitionSpec as P


H = 8
NBR = 4
F32 = jnp.float32
BF16 = jnp.bfloat16


def attention_kernel(near_ref, q_ref, c_ref, kv_ref, far_ref, tile_ref,
                     att_ref, dq_ref, dnear_ref, dfar_ref, acc_ref, bias_ref):
    step = pl.program_id(0)
    block_size, width = q_ref.shape[1], q_ref.shape[2]
    head_dim = width // H
    pair = 2 * head_dim
    scale = head_dim ** (-0.5)

    @pl.when(step == 0)
    def _():
        acc_ref[...] = jnp.zeros_like(acc_ref)

    for j in range(NBR):
        bias_ref[:, j * block_size:(j + 1) * block_size] = jnp.where(tile_ref[0, j] != 0, 0.0, -1e30).astype(F32)
    bias_ref[:, NBR * block_size:] = jnp.zeros((block_size, block_size), F32)
    ids = [near_ref[step * NBR + j] for j in range(NBR)]
    first = lax.broadcasted_iota(jnp.int32, (block_size, pair), 1) < head_dim

    def stacked(x):
        zero = jnp.zeros_like(x)
        return jnp.concatenate([jnp.where(first, x, zero), jnp.where(first, zero, x)], axis=0)

    def joined(column):
        cols = pl.ds(column, pair)
        return jnp.concatenate([kv_ref[i, :, cols] for i in ids] + [far_ref[0, :, cols]], axis=0)

    last = (((1,), (1,)), ((), ()))
    lead = (((0,), (0,)), ((), ()))
    for p in range(H // 2):
        low = p * pair
        cols = slice(low, low + pair)
        query = stacked(q_ref[0, :, cols].astype(F32) * scale).astype(BF16)
        cot_pair = c_ref[0, :, cols].astype(F32)
        cot32 = stacked(cot_pair)
        cot = cot32.astype(BF16)
        keys = joined(low)
        values = joined(width + low)
        scores = lax.dot_general(query, keys, last, preferred_element_type=F32)
        bias = bias_ref[...]
        scores = scores + jnp.concatenate([bias, bias], axis=0)
        peak = jnp.max(scores, axis=-1, keepdims=True)
        weight = jnp.exp(scores - peak)
        total = jnp.sum(weight, axis=-1, keepdims=True)
        probs = weight * (1.0 / total)
        low_probs = probs.astype(BF16)
        att2 = jnp.dot(low_probs, values, preferred_element_type=F32).astype(BF16).astype(F32)
        att_ref[0, :, cols] = jnp.where(first, att2[:block_size], att2[block_size:]).astype(BF16)
        delta = jnp.sum(cot32 * att2, axis=-1, keepdims=True)
        grad_probs = lax.dot_general(cot, values, last, preferred_element_type=F32)
        dscores = (probs * (grad_probs - delta)).astype(BF16)
        dq2 = jnp.dot(dscores, keys, preferred_element_type=F32) * scale
        dq_ref[0, :, cols] = jnp.where(first, dq2[:block_size], dq2[block_size:]).astype(BF16)
        dk = lax.dot_general(query, dscores, lead, preferred_element_type=F32)
        dv = lax.dot_general(cot, low_probs, lead, preferred_element_type=F32)
        for base, grad in ((low, dk), (width + low, dv)):
            rows = pl.ds(base, pair)
            for j in range(NBR):
                acc_ref[ids[j], rows, :] += grad[:, j * block_size:(j + 1) * block_size]
            dfar_ref[0, rows, :] = grad[:, NBR * block_size:].astype(BF16)

    @pl.when(step == pl.num_programs(0) - 1)
    def _():
        dnear_ref[...] = acc_ref[...].astype(BF16)


def attention(near_ids, offset, query, cot, kv, kv_far, tiles):
    own, block_size, width = query.shape
    blocks = kv.shape[0]
    scalars = jnp.concatenate([near_ids.reshape(-1), offset.reshape(1)])
    count = own * NBR
    row = lambda b, s: (b, 0, 0)
    whole = lambda b, s: (0, 0, 0)
    grid_spec = pltpu.PrefetchScalarGridSpec(
        num_scalar_prefetch=1,
        grid=(own,),
        in_specs=[
            pl.BlockSpec((1, block_size, width), row),
            pl.BlockSpec((1, block_size, width), row),
            pl.BlockSpec((blocks, block_size, 2 * width), whole),
            pl.BlockSpec((1, block_size, 2 * width), row),
            pl.BlockSpec((1, NBR, block_size, block_size), lambda b, s: (s[count] + b, 0, 0, 0)),
        ],
        out_specs=[
            pl.BlockSpec((1, block_size, width), row),
            pl.BlockSpec((1, block_size, width), row),
            pl.BlockSpec((blocks, 2 * width, block_size), whole),
            pl.BlockSpec((1, 2 * width, block_size), row),
        ],
        scratch_shapes=[
            pltpu.VMEM((blocks, 2 * width, block_size), F32),
            pltpu.VMEM((block_size, (NBR + 1) * block_size), F32),
        ],
    )
    flops = 12 * own * H * block_size * (NBR + 1) * block_size * (width // H)
    return pl.pallas_call(
        attention_kernel,
        grid_spec=grid_spec,
        out_shape=[
            jax.ShapeDtypeStruct((own, block_size, width), BF16),
            jax.ShapeDtypeStruct((own, block_size, width), BF16),
            jax.ShapeDtypeStruct((blocks, 2 * width, block_size), BF16),
            jax.ShapeDtypeStruct((own, 2 * width, block_size), BF16),
        ],
        compiler_params=pltpu.CompilerParams(vmem_limit_bytes=56 * 1024 * 1024),
        cost_estimate=pl.CostEstimate(
            flops=8 * flops,
            bytes_accessed=20 * own * block_size * width,
            transcendentals=own * H * block_size * (NBR + 1) * block_size,
        ),
        name="attention",
    )(scalars, query, cot, kv, kv_far, tiles)


def layer(node_feats, w_qkv, w_out, neighbours, tiles, partner, layer_cot):
    rows, width = node_feats.shape
    parts = lax.axis_size("dom")
    groups = lax.axis_size("head")
    me = lax.axis_index("head")
    blocks = partner.shape[0]
    block_size = tiles.shape[2]
    own = blocks // groups
    half = block_size // 2
    span = width // groups
    slots = (blocks + parts - 2) // (parts - 1)
    swap = [(0, 1), (1, 0)]

    def pick(x, i):
        return lax.dynamic_index_in_dim(x, i, 1, keepdims=False)

    def halves(mine, other):
        both = jnp.stack([mine, other], axis=1)
        flip = jnp.stack([other, mine], axis=1)
        return jnp.where(me == 0, both, flip).reshape(mine.shape[0], block_size, -1)

    target = partner // blocks
    iota = jnp.arange(blocks, dtype=jnp.int32)
    same = target[:, None] == target[None, :]
    earlier = iota[None, :] < iota[:, None]
    lower = partner[None, :] < partner[:, None]
    order = (iota + own * me) % blocks
    send_slot = (target * slots + jnp.sum((same & earlier).astype(jnp.int32), axis=1))[order]
    recv_slot = (target * slots + jnp.sum((same & lower).astype(jnp.int32), axis=1))[order]
    all_slots = jnp.arange(parts * slots, dtype=jnp.int32)
    send_from = jnp.sum(jnp.where(send_slot[None, :] == all_slots[:, None], iota[None, :], 0), axis=1)
    recv_from = jnp.sum(jnp.where(recv_slot[None, :] == all_slots[:, None], iota[None, :], 0), axis=1)

    feats = node_feats.reshape(own, 2, half, width)
    peer_a = lax.ppermute(pick(feats, 1 - me), "head", swap)
    peer_b = lax.ppermute(pick(feats, me), "head", swap)
    half_feats = jnp.concatenate([pick(feats, me), peer_a], axis=0)
    incoming = lax.all_to_all(half_feats[send_from], "dom", split_axis=0, concat_axis=0, tiled=True)
    half_far = incoming[recv_slot]
    other_far = lax.ppermute(half_far[own:], "head", swap)
    feats_far = halves(half_far[:own], other_far)
    feats_peer = halves(peer_a, peer_b)

    w_split = w_qkv.reshape(width, groups, 3, span).transpose(0, 2, 1, 3).reshape(width, 3 * width)
    w_query, w_kv = w_split[:, :width], w_split[:, width:]

    def project(x, w):
        return jnp.dot(x, w, preferred_element_type=F32).astype(BF16)

    query = project(node_feats, w_query).reshape(own, block_size, width)
    cot = project(layer_cot, w_out.T).reshape(own, block_size, width)
    feats_near = jnp.concatenate([node_feats, feats_peer.reshape(rows, width)], axis=0)
    feats_far = feats_far.reshape(rows, width)
    kv = project(feats_near, w_kv).reshape(blocks, block_size, 2 * width)
    kv_far = project(feats_far, w_kv).reshape(own, block_size, 2 * width)
    near_ids = lax.dynamic_slice_in_dim(neighbours, me * own, own, 0)
    near_ids = (near_ids + own * me) % blocks
    attended, dq, dnear, dfar = attention(near_ids, me * own, query, cot, kv, kv_far, tiles)

    attended = attended.reshape(rows, width)
    dq = dq.reshape(rows, width)

    def back(x):
        return jnp.einsum("bcn,dc->bnd", x, w_kv, preferred_element_type=F32)

    place = lax.axis_index("dom")

    def rows_in(spec, a, b):
        return jnp.einsum(spec, a, b, preferred_element_type=F32)

    near_rows = feats_near.reshape(blocks, block_size, width)
    far_rows = feats_far.reshape(own, block_size, width)

    far_grad = back(dfar).astype(BF16).reshape(own, 2, half, width)
    far_peer = lax.ppermute(pick(far_grad, 1 - me), "head", swap)
    dw_q = rows_in("rd,rc->dc", node_feats, dq)
    dw_kv = rows_in("bnd,bcn->dc", near_rows, dnear) + rows_in("bnd,bcn->dc", far_rows, dfar)
    dw_out = rows_in("rc,rd->cd", layer_cot, attended)
    pieces = (dw_q, dw_kv[:, :width], dw_kv[:, width:], dw_out)
    dw_all = jnp.stack(
        [jnp.concatenate([x[:, g * span:(g + 1) * span] for x in pieces], axis=1) for g in range(groups)]
    )
    peer_grad = back(dnear[own:]).reshape(own, 2, half, width)
    far_peer, dw_all = lax.optimization_barrier((far_peer, dw_all))
    half_grad = jnp.concatenate([pick(far_grad, me), far_peer], axis=0)
    returned = lax.all_to_all(half_grad[recv_from], "dom", split_axis=0, concat_axis=0, tiled=True)

    def halve(x, axis, bit, name, pairs):
        take = lambda i: lax.dynamic_index_in_dim(x, i, axis, keepdims=False)
        got = lax.ppermute(take(1 - bit).astype(BF16), name, pairs)
        return take(bit) + got.astype(F32)

    def dom_stage(x, k, axis):
        pairs = [(i, i ^ (1 << k)) for i in range(parts)]
        shape = x.shape[:axis] + (x.shape[axis] // 2, 2) + x.shape[axis + 1:]
        return halve(x.reshape(shape), axis + 1, (place >> k) & 1, "dom", pairs)

    dw_sum = dom_stage(dw_all.reshape(groups, parts, width // parts, 4 * span), 0, 1)
    dw_sum = halve(dw_sum, 0, me, "head", swap)
    early = lax.ppermute(pick(peer_grad, 1 - me).astype(BF16), "head", swap)
    dw_sum = dom_stage(dw_sum, 1, 0)
    returned, dw_sum = lax.optimization_barrier((returned, dw_sum))

    returned = returned[send_slot].astype(F32)
    late = lax.ppermute((pick(peer_grad, me) + returned[own:]).astype(BF16), "head", swap)
    for k in range(2, parts.bit_length() - 1):
        dw_sum = dom_stage(dw_sum, k, 0)
    dw_sum = dw_sum[0]

    layer_out = project(attended, w_out)
    own_grad = (
        jnp.einsum("rc,dc->rd", dq, w_query, preferred_element_type=F32).reshape(own, block_size, width)
        + back(dnear[:own])
    )
    feat_grad = own_grad + halves(returned[:own] + early.astype(F32), late.astype(F32))
    feat_grad = feat_grad.astype(BF16).reshape(rows, width)
    return (layer_out, feat_grad, dw_sum[:, : 3 * span], dw_sum[:, 3 * span:].T)


def solution(mesh):
    placed = (
        P(("dom", "head"), None),
        P(),
        P(),
        P("dom", None),
        P("dom", None, None, None),
        P("dom"),
        P(("dom", "head"), None),
    )
    return jax.shard_map(
        layer,
        mesh=mesh,
        in_specs=placed,
        out_specs=(
            P(("dom", "head"), None),
            P(("dom", "head"), None),
            P("dom", "head"),
            P("head", "dom"),
        ),
        check_vma=False,
    )
```

```python
import jax
import jax.numpy as jnp
from jax import lax
from jax.experimental import pallas as pl
from jax.experimental.pallas import tpu as pltpu
from jax.sharding import PartitionSpec as P


H = 8
NBR = 4
F32 = jnp.float32
BF16 = jnp.bfloat16


def attention_kernel(near_ref, q_ref, c_ref, kv_ref, far_ref, tile_ref,
                     att_ref, dq_ref, dnear_ref, dfar_ref, acc_ref, bias_ref):
    step = pl.program_id(0)
    block_size, width = q_ref.shape[1], q_ref.shape[2]
    head_dim = width // H
    pair = 2 * head_dim
    scale = head_dim ** (-0.5)

    @pl.when(step == 0)
    def _():
        acc_ref[...] = jnp.zeros_like(acc_ref)

    for j in range(NBR):
        bias_ref[:, j * block_size:(j + 1) * block_size] = jnp.where(tile_ref[0, j] != 0, 0.0, -1e30).astype(F32)
    bias_ref[:, NBR * block_size:] = jnp.zeros((block_size, block_size), F32)
    ids = [near_ref[step * NBR + j] for j in range(NBR)]
    first = lax.broadcasted_iota(jnp.int32, (block_size, pair), 1) < head_dim

    def stacked(x):
        zero = jnp.zeros_like(x)
        return jnp.concatenate([jnp.where(first, x, zero), jnp.where(first, zero, x)], axis=0)

    def joined(column):
        cols = pl.ds(column, pair)
        return jnp.concatenate([kv_ref[i, :, cols] for i in ids] + [far_ref[0, :, cols]], axis=0)

    last = (((1,), (1,)), ((), ()))
    lead = (((0,), (0,)), ((), ()))
    for p in range(H // 2):
        low = p * pair
        cols = slice(low, low + pair)
        query = stacked(q_ref[0, :, cols].astype(F32) * scale).astype(BF16)
        cot_pair = c_ref[0, :, cols].astype(F32)
        cot32 = stacked(cot_pair)
        cot = cot32.astype(BF16)
        keys = joined(low)
        values = joined(width + low)
        scores = lax.dot_general(query, keys, last, preferred_element_type=F32)
        bias = bias_ref[...]
        scores = scores + jnp.concatenate([bias, bias], axis=0)
        peak = jnp.max(scores, axis=-1, keepdims=True)
        weight = jnp.exp(scores - peak)
        total = jnp.sum(weight, axis=-1, keepdims=True)
        probs = weight * (1.0 / total)
        low_probs = probs.astype(BF16)
        att2 = jnp.dot(low_probs, values, preferred_element_type=F32).astype(BF16).astype(F32)
        att_ref[0, :, cols] = jnp.where(first, att2[:block_size], att2[block_size:]).astype(BF16)
        delta = jnp.sum(cot32 * att2, axis=-1, keepdims=True)
        grad_probs = lax.dot_general(cot, values, last, preferred_element_type=F32)
        dscores = (probs * (grad_probs - delta)).astype(BF16)
        dq2 = jnp.dot(dscores, keys, preferred_element_type=F32) * scale
        dq_ref[0, :, cols] = jnp.where(first, dq2[:block_size], dq2[block_size:]).astype(BF16)
        dk = lax.dot_general(query, dscores, lead, preferred_element_type=F32)
        dv = lax.dot_general(cot, low_probs, lead, preferred_element_type=F32)
        for base, grad in ((low, dk), (width + low, dv)):
            rows = pl.ds(base, pair)
            for j in range(NBR):
                acc_ref[ids[j], rows, :] += grad[:, j * block_size:(j + 1) * block_size]
            dfar_ref[0, rows, :] = grad[:, NBR * block_size:].astype(BF16)

    @pl.when(step == pl.num_programs(0) - 1)
    def _():
        dnear_ref[...] = acc_ref[...].astype(BF16)


def attention(near_ids, offset, query, cot, kv, kv_far, tiles):
    own, block_size, width = query.shape
    blocks = kv.shape[0]
    scalars = jnp.concatenate([near_ids.reshape(-1), offset.reshape(1)])
    count = own * NBR
    row = lambda b, s: (b, 0, 0)
    whole = lambda b, s: (0, 0, 0)
    grid_spec = pltpu.PrefetchScalarGridSpec(
        num_scalar_prefetch=1,
        grid=(own,),
        in_specs=[
            pl.BlockSpec((1, block_size, width), row),
            pl.BlockSpec((1, block_size, width), row),
            pl.BlockSpec((blocks, block_size, 2 * width), whole),
            pl.BlockSpec((1, block_size, 2 * width), row),
            pl.BlockSpec((1, NBR, block_size, block_size), lambda b, s: (s[count] + b, 0, 0, 0)),
        ],
        out_specs=[
            pl.BlockSpec((1, block_size, width), row),
            pl.BlockSpec((1, block_size, width), row),
            pl.BlockSpec((blocks, 2 * width, block_size), whole),
            pl.BlockSpec((1, 2 * width, block_size), row),
        ],
        scratch_shapes=[
            pltpu.VMEM((blocks, 2 * width, block_size), F32),
            pltpu.VMEM((block_size, (NBR + 1) * block_size), F32),
        ],
    )
    flops = 12 * own * H * block_size * (NBR + 1) * block_size * (width // H)
    return pl.pallas_call(
        attention_kernel,
        grid_spec=grid_spec,
        out_shape=[
            jax.ShapeDtypeStruct((own, block_size, width), BF16),
            jax.ShapeDtypeStruct((own, block_size, width), BF16),
            jax.ShapeDtypeStruct((blocks, 2 * width, block_size), BF16),
            jax.ShapeDtypeStruct((own, 2 * width, block_size), BF16),
        ],
        compiler_params=pltpu.CompilerParams(vmem_limit_bytes=56 * 1024 * 1024),
        cost_estimate=pl.CostEstimate(
            flops=8 * flops,
            bytes_accessed=20 * own * block_size * width,
            transcendentals=own * H * block_size * (NBR + 1) * block_size,
        ),
        name="attention",
    )(scalars, query, cot, kv, kv_far, tiles)


def layer(node_feats, w_qkv, w_out, neighbours, tiles, partner, layer_cot):
    rows, width = node_feats.shape
    parts = lax.axis_size("dom")
    groups = lax.axis_size("head")
    me = lax.axis_index("head")
    blocks = partner.shape[0]
    block_size = tiles.shape[2]
    own = blocks // groups
    half = block_size // 2
    span = width // groups
    slots = (blocks + parts - 2) // (parts - 1)
    swap = [(0, 1), (1, 0)]

    def pick(x, i):
        return lax.dynamic_index_in_dim(x, i, 1, keepdims=False)

    def halves(mine, other):
        both = jnp.stack([mine, other], axis=1)
        flip = jnp.stack([other, mine], axis=1)
        return jnp.where(me == 0, both, flip).reshape(mine.shape[0], block_size, -1)

    target = partner // blocks
    iota = jnp.arange(blocks, dtype=jnp.int32)
    same = target[:, None] == target[None, :]
    earlier = iota[None, :] < iota[:, None]
    lower = partner[None, :] < partner[:, None]
    order = (iota + own * me) % blocks
    send_slot = (target * slots + jnp.sum((same & earlier).astype(jnp.int32), axis=1))[order]
    recv_slot = (target * slots + jnp.sum((same & lower).astype(jnp.int32), axis=1))[order]
    all_slots = jnp.arange(parts * slots, dtype=jnp.int32)
    send_from = jnp.sum(jnp.where(send_slot[None, :] == all_slots[:, None], iota[None, :], 0), axis=1)
    recv_from = jnp.sum(jnp.where(recv_slot[None, :] == all_slots[:, None], iota[None, :], 0), axis=1)

    feats = node_feats.reshape(own, 2, half, width)
    split = [slice(c * width // 2, (c + 1) * width // 2) for c in range(2)]
    mine, give = pick(feats, me), pick(feats, 1 - me)

    def over_dom(x, source):
        return lax.all_to_all(x[source], "dom", split_axis=0, concat_axis=0, tiled=True)

    a_pieces = [lax.ppermute(give[:, :, c], "head", swap) for c in split]
    far_mine, far_other = [], []
    for c, got in zip(split, a_pieces):
        piece = over_dom(jnp.concatenate([mine[:, :, c], got], axis=0), send_from)[recv_slot]
        far_mine.append(piece[:own])
        far_other.append(lax.ppermute(piece[own:], "head", swap))
    later, _ = lax.optimization_barrier((mine, a_pieces[1]))
    peer_b = lax.ppermute(later, "head", swap)
    peer_a = jnp.concatenate(a_pieces, axis=2)
    feats_far = halves(jnp.concatenate(far_mine, axis=2), jnp.concatenate(far_other, axis=2))
    feats_peer = halves(peer_a, peer_b)

    w_split = w_qkv.reshape(width, groups, 3, span).transpose(0, 2, 1, 3).reshape(width, 3 * width)
    w_query, w_kv = w_split[:, :width], w_split[:, width:]

    def project(x, w):
        return jnp.dot(x, w, preferred_element_type=F32).astype(BF16)

    query = project(node_feats, w_query).reshape(own, block_size, width)
    cot = project(layer_cot, w_out.T).reshape(own, block_size, width)
    feats_near = jnp.concatenate([node_feats, feats_peer.reshape(rows, width)], axis=0)
    feats_far = feats_far.reshape(rows, width)
    kv = project(feats_near, w_kv).reshape(blocks, block_size, 2 * width)
    kv_far = project(feats_far, w_kv).reshape(own, block_size, 2 * width)
    near_ids = lax.dynamic_slice_in_dim(neighbours, me * own, own, 0)
    near_ids = (near_ids + own * me) % blocks
    attended, dq, dnear, dfar = attention(near_ids, me * own, query, cot, kv, kv_far, tiles)

    attended = attended.reshape(rows, width)
    dq = dq.reshape(rows, width)

    def back(x):
        return jnp.einsum("bcn,dc->bnd", x, w_kv, preferred_element_type=F32)

    place = lax.axis_index("dom")

    def rows_in(spec, a, b):
        return jnp.einsum(spec, a, b, preferred_element_type=F32)

    near_rows = feats_near.reshape(blocks, block_size, width)
    far_rows = feats_far.reshape(own, block_size, width)

    far_grad = back(dfar).astype(BF16).reshape(own, 2, half, width)
    far_own, far_give = pick(far_grad, me), pick(far_grad, 1 - me)
    far_peer0 = lax.ppermute(far_give[:, :, split[0]], "head", swap)
    far_peer = lax.ppermute(far_give[:, :, split[1]], "head", swap)
    dw_q = rows_in("rd,rc->dc", node_feats, dq)
    dw_kv = rows_in("bnd,bcn->dc", near_rows, dnear) + rows_in("bnd,bcn->dc", far_rows, dfar)
    dw_out = rows_in("rc,rd->cd", layer_cot, attended)
    pieces = (dw_q, dw_kv[:, :width], dw_kv[:, width:], dw_out)
    dw_all = jnp.stack(
        [jnp.concatenate([x[:, g * span:(g + 1) * span] for x in pieces], axis=1) for g in range(groups)]
    )
    peer_grad = back(dnear[own:]).reshape(own, 2, half, width)
    far_peer, dw_all = lax.optimization_barrier((far_peer, dw_all))
    returned0 = over_dom(jnp.concatenate([far_own[:, :, split[0]], far_peer0], axis=0), recv_from)
    returned = over_dom(jnp.concatenate([far_own[:, :, split[1]], far_peer], axis=0), recv_from)

    def halve(x, axis, bit, name, pairs):
        take = lambda i: lax.dynamic_index_in_dim(x, i, axis, keepdims=False)
        got = lax.ppermute(take(1 - bit).astype(BF16), name, pairs)
        return take(bit) + got.astype(F32)

    def dom_stage(x, k, axis):
        pairs = [(i, i ^ (1 << k)) for i in range(parts)]
        shape = x.shape[:axis] + (x.shape[axis] // 2, 2) + x.shape[axis + 1:]
        return halve(x.reshape(shape), axis + 1, (place >> k) & 1, "dom", pairs)

    dw_sum = dom_stage(dw_all.reshape(groups, parts, width // parts, 4 * span), 0, 1)
    dw_sum = halve(dw_sum, 0, me, "head", swap)
    early = lax.ppermute(pick(peer_grad, 1 - me).astype(BF16), "head", swap)
    dw_sum = dom_stage(dw_sum, 1, 0)
    late_near = pick(peer_grad, me)
    late_second = late_near[:, :, split[1]]
    returned, dw_sum, late_second = lax.optimization_barrier((returned, dw_sum, late_second))

    late_pieces = (late_near[:, :, split[0]], late_second)
    back_pieces = [x[send_slot].astype(F32) for x in (returned0, returned)]
    late = jnp.concatenate(
        [
            lax.ppermute((near + x[own:]).astype(BF16), "head", swap)
            for near, x in zip(late_pieces, back_pieces)
        ],
        axis=2,
    )
    returned = jnp.concatenate([x[:own] for x in back_pieces], axis=2)
    for k in range(2, parts.bit_length() - 1):
        dw_sum = dom_stage(dw_sum, k, 0)
    dw_sum = dw_sum[0]

    layer_out = project(attended, w_out)
    own_grad = (
        jnp.einsum("rc,dc->rd", dq, w_query, preferred_element_type=F32).reshape(own, block_size, width)
        + back(dnear[:own])
    )
    feat_grad = own_grad + halves(returned + early.astype(F32), late.astype(F32))
    feat_grad = feat_grad.astype(BF16).reshape(rows, width)
    return (layer_out, feat_grad, dw_sum[:, : 3 * span], dw_sum[:, 3 * span:].T)


def solution(mesh):
    placed = (
        P(("dom", "head"), None),
        P(),
        P(),
        P("dom", None),
        P("dom", None, None, None),
        P("dom"),
        P(("dom", "head"), None),
    )
    return jax.shard_map(
        layer,
        mesh=mesh,
        in_specs=placed,
        out_specs=(
            P(("dom", "head"), None),
            P(("dom", "head"), None),
            P("dom", "head"),
            P("head", "dom"),
        ),
        check_vma=False,
    )
```
